32 devices in a mesh: groups: 2 (over y), row: 4 (over x, core), col: 4 (over z).
Axes of the slice: x: 2, y: 2, z: 4, core: 2. Of those that a mesh axis runs over, the one named last changes fastest.
Arguments:
- tiles: float32 [512, 128, 128], P(('groups', 'row', 'col')), parts along dimension 0, may hold values from 0 to 9
- tile_index: int32 [512, 2], P(('groups', 'row', 'col')), parts along dimension 0, may hold values from 0 to 3, as said below
- tile_count: int32 [32], P(('groups', 'row', 'col')), parts along dimension 0, may hold values from 4 to 16, as said below
- sources: int32 [16], P('groups'), parts along dimension 0, may hold values from 0 to 2047
Outputs:
- distance: float32 [16, 2048], P('groups', ('row', 'col')), parts along dimension 0
- path_counts: float32 [16, 2048], P('groups', ('row', 'col')), parts along dimension 0
- centrality: float32 [4096], P(('groups', 'row', 'col')), parts along dimension 0
The draws below stay inside these ranges and needn't reach their ends.
There are 2 independent parts, one for each index of `groups`. The reference program is written for one: setup_inputs(seed, part) draws one part's arguments, and reference() takes and returns one part's arrays. A program takes and returns all parts, laid end to end along the dimension named above; each array names one. Nothing has to cross between parts.
Inputs may be any that keep to these rules, and one draw needn't show every extreme that they name: `tile_index`: entry (r, c) of a slot has r below 4 and c below 4; the 16 slots of one device name distinct pairs. `tile_count`: one entry per device; slots of a device from its count on hold only zeros; some device has all 16 slots live.
All inputs are finite; a program needn't handle non-finite values.
Results may differ from the reference program's by a relative error of at most 0.0003.
Values sent between devices are 32-bit elements; how exact they have to be, the bound alone decides.
A program may use at most 64 MiB of HBM per device.

```python
import jax
import jax.numpy as jnp
from jax import lax

TILE = 128
SLOTS = 16
SOURCES = 8
WMAX = 8
LEVELS = 3
BACK = 2
DEVS = 16
VERTICES = 2048
SLOT_ALL = 256
N_ROW = 4
N_COL = 4


def tile_layout(key):
    layout_key = jax.random.fold_in(key, 101)
    perm_key, count_key, pick_key, weight_key, keep_key, level_key = jax.random.split(layout_key, 6)
    placed = jax.vmap(lambda one_key: jax.random.permutation(one_key, N_ROW * N_COL)[:SLOTS])(jax.random.split(perm_key, DEVS))
    live_counts = jax.random.randint(count_key, (DEVS,), SLOTS // 4, SLOTS + 1)
    fullest = jax.random.randint(pick_key, (), 0, DEVS)
    live_counts = jnp.where(jnp.arange(DEVS) == fullest, SLOTS, live_counts).astype(jnp.int32)
    whole_parts = jax.random.randint(weight_key, (DEVS, SLOTS, TILE, TILE), 1, WMAX + 1).astype(jnp.float32)
    kept_edges = jax.random.randint(keep_key, (DEVS, SLOTS, TILE, TILE), 0, TILE) < 2
    live_slots = jnp.arange(SLOTS)[None, :] < live_counts[:, None]
    vertex_level = jax.random.randint(level_key, (VERTICES,), 0, 2 ** 17).astype(jnp.float32) * 2.0 ** (-18)
    row_tile = placed // N_ROW
    col_tile = placed % N_ROW
    dev_ids = jnp.arange(DEVS)
    row_base = (dev_ids[:, None] // N_COL * N_COL + row_tile) * TILE
    col_base = (col_tile * N_COL + dev_ids[:, None] % N_COL) * TILE
    offsets = jnp.arange(TILE)
    row_level = vertex_level[row_base[:, :, None] + offsets[None, None, :]]
    col_level = vertex_level[col_base[:, :, None] + offsets[None, None, :]]
    weights = whole_parts + col_level[:, :, None, :] - row_level[:, :, :, None]
    tile_values = jnp.where(kept_edges & live_slots[:, :, None, None], weights, 0.0).reshape(DEVS * SLOTS, TILE, TILE).astype(jnp.float32)
    positions = jnp.stack([row_tile, col_tile], axis=-1).reshape(DEVS * SLOTS, 2).astype(jnp.int32)
    return (tile_values, positions, live_counts)


def draw_tiles(key, part):
    return tile_layout(key)[0]


def draw_tile_index(key, part):
    return tile_layout(key)[1]


def draw_tile_count(key, part):
    return tile_layout(key)[2]


def place_ends(drawn, own_key, low, high):
    longest = drawn.shape.index(max(drawn.shape))
    spots = []
    for shift in (0, 1):
        where = [jax.random.randint(jax.random.fold_in(own_key, axis), (), 0, length) for axis, length in enumerate(drawn.shape)]
        where[longest] = (where[longest] + shift) % drawn.shape[longest]
        spots.append(tuple(where))
    return drawn.at[spots[0]].set(low).at[spots[1]].set(high)


def setup_inputs(seed: int = 0, part: int = 0) -> dict:
    seeds = jax.random.split(jax.random.key(seed), 5)
    part_splits = jax.random.split(jax.random.fold_in(seeds[4], part), 5)
    tiles = draw_tiles(jax.random.fold_in(jax.random.fold_in(seeds[4], part), 71), part)
    tile_index = draw_tile_index(jax.random.fold_in(jax.random.fold_in(seeds[4], part), 71), part)
    tile_count = draw_tile_count(jax.random.fold_in(jax.random.fold_in(seeds[4], part), 71), part)
    sources = place_ends(jax.random.randint(part_splits[3], (SOURCES,), 0, VERTICES), jax.random.fold_in(part_splits[3], 1), 0, VERTICES - 1).astype(jnp.int32)
    return {"tiles": tiles, "tile_index": tile_index, "tile_count": tile_count, "sources": sources}


far_value = 1.0e6
no_edge = 2.0e6


def combine_pair(left_pair, right_pair):
    best_dist = jnp.minimum(left_pair[0], right_pair[0])
    total_count = jnp.where(left_pair[0] == best_dist, left_pair[1], 0.0) + jnp.where(right_pair[0] == best_dist, right_pair[1], 0.0)
    return best_dist, total_count


def edge_weights(raw_tile):
    return jnp.where(raw_tile > 0, raw_tile.astype(jnp.float32), no_edge)


def relax_tile(near_dist, near_count, weight_tile):
    source_rows = near_dist.shape[0]
    tile_side = weight_tile.shape[0]
    block_size = min(16, tile_side)
    blocks = tile_side // block_size
    dist_blocks = near_dist.reshape(source_rows, blocks, block_size).transpose(1, 0, 2)
    count_blocks = near_count.reshape(source_rows, blocks, block_size).transpose(1, 0, 2)
    weight_blocks = weight_tile.reshape(blocks, block_size, tile_side)

    def advance(carried, pieces):
        dist_part, count_part, weight_part = pieces
        reached = dist_part[:, :, None] + weight_part[None, :, :]
        best_dist = jnp.min(reached, axis=1)
        total_count = jnp.sum(jnp.where(reached == best_dist[:, None, :], count_part[:, :, None], 0.0), axis=1)
        return combine_pair(carried, (best_dist, total_count)), None

    initial = (jnp.full((source_rows, tile_side), far_value, near_dist.dtype), jnp.zeros((source_rows, tile_side), near_dist.dtype))
    result, unused = lax.scan(advance, initial, (dist_blocks, count_blocks, weight_blocks))
    return result


def depend_tile(upper_dist, lower_dist, lower_coef, weight_tile):
    source_rows = upper_dist.shape[0]
    tile_side = weight_tile.shape[0]
    block_size = min(16, tile_side)
    blocks = tile_side // block_size
    upper_blocks = upper_dist.reshape(source_rows, blocks, block_size).transpose(1, 0, 2)
    weight_blocks = weight_tile.reshape(blocks, block_size, tile_side)

    def dependency_rows(pieces):
        upper_part, weight_part = pieces
        reached = upper_part[:, :, None] + weight_part[None, :, :]
        return jnp.sum(jnp.where(reached == lower_dist[:, None, :], lower_coef[:, None, :], 0.0), axis=2)

    row_parts = lax.map(dependency_rows, (upper_blocks, weight_blocks))
    return row_parts.transpose(1, 0, 2).reshape(source_rows, tile_side)


def reference(tiles, tile_index, tile_count, sources):
    source_rows = sources.shape[0]
    vertex_ids = jnp.arange(VERTICES, dtype=jnp.int32)
    is_source = vertex_ids[None, :] == sources[:, None]
    start_dist = jnp.where(is_source, 0.0, far_value).astype(jnp.float32)
    source_ones = jnp.where(is_source, 1.0, 0.0).astype(jnp.float32)
    distance = start_dist
    path_counts = source_ones
    slot_ids = jnp.arange(SLOT_ALL, dtype=jnp.int32)

    def place(slot_id):
        owner_dev = slot_id // SLOTS
        local_slot = slot_id % SLOTS
        row_block = owner_dev // N_COL
        col_block = owner_dev % N_COL
        row_start = ((row_block * N_COL + tile_index[slot_id, 0]) * TILE).astype(jnp.int32)
        col_start = ((tile_index[slot_id, 1] * N_COL + col_block) * TILE).astype(jnp.int32)
        return row_start, col_start, local_slot < tile_count[owner_dev]

    for level_no in range(LEVELS):
        def forward_step(carried, slot_id, distance=distance, path_counts=path_counts):
            row_start, col_start, is_live = place(slot_id)
            weight_tile = edge_weights(tiles[slot_id])

            def active(current):
                near_dist = lax.dynamic_slice_in_dim(distance, row_start, TILE, 1)
                near_count = lax.dynamic_slice_in_dim(path_counts, row_start, TILE, 1)
                found = relax_tile(near_dist, near_count, weight_tile)
                previous = (lax.dynamic_slice_in_dim(current[0], col_start, TILE, 1), lax.dynamic_slice_in_dim(current[1], col_start, TILE, 1))
                merged = combine_pair(previous, found)
                return (lax.dynamic_update_slice_in_dim(current[0], merged[0], col_start, 1), lax.dynamic_update_slice_in_dim(current[1], merged[1], col_start, 1))

            return lax.cond(is_live, active, lambda unchanged: unchanged, carried), None

        initial = (jnp.full((source_rows, VERTICES), far_value, jnp.float32), jnp.zeros((source_rows, VERTICES), jnp.float32))
        (cand_dist, cand_count), unused = lax.scan(forward_step, initial, slot_ids)
        distance = jnp.minimum(start_dist, cand_dist)
        path_counts = source_ones + jnp.where(cand_dist == distance, cand_count, 0.0)

    dependency = jnp.zeros((source_rows, VERTICES), jnp.float32)
    for back_no in range(BACK):
        coefficient = jnp.where(path_counts > 0.5, (1.0 + dependency) / jnp.maximum(path_counts, 1.0), 0.0)

        def backward_step(carried, slot_id, coefficient=coefficient):
            row_start, col_start, is_live = place(slot_id)
            weight_tile = edge_weights(tiles[slot_id])

            def active(current):
                upper_dist = lax.dynamic_slice_in_dim(distance, row_start, TILE, 1)
                lower_dist = lax.dynamic_slice_in_dim(distance, col_start, TILE, 1)
                lower_coef = lax.dynamic_slice_in_dim(coefficient, col_start, TILE, 1)
                dep_term = depend_tile(upper_dist, lower_dist, lower_coef, weight_tile)
                previous = lax.dynamic_slice_in_dim(current, row_start, TILE, 1)
                return lax.dynamic_update_slice_in_dim(current, previous + dep_term, row_start, 1)

            return lax.cond(is_live, active, lambda unchanged: unchanged, carried), None

        accumulated, unused = lax.scan(backward_step, jnp.zeros((source_rows, VERTICES), jnp.float32), slot_ids)
        dependency = path_counts * accumulated

    centrality = jnp.sum(jnp.where(is_source, 0.0, dependency), axis=0) / source_rows
    shown = jnp.where(distance < 0.5 * far_value, distance, -1.0)
    return shown, path_counts, centrality
```

```python
import functools

import jax
import jax.numpy as jnp
from jax import lax
from jax.experimental import pallas as pl
from jax.experimental.pallas import tpu as pltpu
from jax.sharding import PartitionSpec as P

LEVELS = 3
BACK = 2
CHUNK = 4

far_value = 1000000.0
no_edge = 2000000.0
half_far = 500000.0


def partner(me, step, count):
    if count & (count - 1):
        return (me + step) % count
    total = 0
    bit = 1
    while bit < count:
        total = total + ((me // bit) % 2 + (step // bit) % 2) % 2 * bit
        bit *= 2
    return total


def body(
    row_count,
    col_count,
    index_ref,
    count_ref,
    source_ref,
    tiles_ref,
    dist_out,
    path_out,
    cent_out,
    raw,
    place_ref,
    weights,
    weights_back,
    partial,
    merged,
    band,
    lower,
    sums_out,
    sums_in,
    load_sem,
    row_send,
    row_recv,
    col_send,
    col_recv,
):
    slot_total, tile_side = raw.shape[0], raw.shape[1]
    source_rows = dist_out.shape[0]
    my_row = lax.axis_index("row")
    my_col = lax.axis_index("col")
    positions = row_count * col_count
    row_chunk = CHUNK if row_count % CHUNK == 0 else 1
    col_chunk = CHUNK if col_count % CHUNK == 0 else 1
    wide = (source_rows, tile_side)
    pending = []

    load = pltpu.make_async_copy(tiles_ref, raw, load_sem)
    load.start()
    barrier = pltpu.get_barrier_semaphore()
    for axis, me, count in (("row", my_row, row_count), ("col", my_col, col_count)):
        for step in range(1, count):
            pl.semaphore_signal(
                barrier,
                inc=1,
                device_id={axis: partner(me, step, count)},
                device_id_type=pl.DeviceIdType.MESH,
            )

    def push(axis, stage, source_of, target):
        me, count = (my_row, row_count) if axis == "row" else (my_col, col_count)
        send, recv = (row_send, row_recv) if axis == "row" else (col_send, col_recv)
        for step in range(1, count):
            other = partner(me, step, count)
            copy = pltpu.make_async_remote_copy(
                src_ref=source_of(other),
                dst_ref=target,
                send_sem=send.at[stage, step],
                recv_sem=recv.at[stage, me],
                device_id={axis: other},
                device_id_type=pl.DeviceIdType.MESH,
            )
            copy.start()
            pending.append(copy)

    def arrived(axis, stage, other, target):
        send, recv = (row_send, row_recv) if axis == "row" else (col_send, col_recv)
        pltpu.make_async_remote_copy(
            src_ref=target,
            dst_ref=target,
            send_sem=send.at[stage, 0],
            recv_sem=recv.at[stage, other],
            device_id={axis: other},
            device_id_type=pl.DeviceIdType.MESH,
        ).wait_recv()

    live_count = count_ref[0]

    def find_slot(position, carried):
        found = jnp.int32(-1)
        for slot in range(slot_total):
            here = (index_ref[slot, 0] * row_count + index_ref[slot, 1] == position) & (
                slot < live_count
            )
            found = jnp.where(here, jnp.int32(slot), found)
        place_ref[position] = found
        return carried

    lax.fori_loop(0, positions, find_slot, 0)

    lane = lax.broadcasted_iota(jnp.int32, wide, 1)
    sub = lax.broadcasted_iota(jnp.int32, wide, 0)
    own_base = (my_row * col_count + my_col) * tile_side
    wanted = jnp.full(wide, -1, jnp.int32)
    for row in range(source_rows):
        wanted = jnp.where(sub == row, source_ref[row] - own_base, wanted)
    own_source = lane == wanted
    start_dist = jnp.where(own_source, 0.0, far_value).astype(jnp.float32)
    source_ones = jnp.where(own_source, 1.0, 0.0).astype(jnp.float32)

    load.wait()

    def prepare(position, carried):
        slot = place_ref[position]
        tile = raw[jnp.maximum(slot, 0)]
        limit = jnp.where(slot >= 0, 0.0, far_value).astype(jnp.float32)
        weights[position] = jnp.where(tile > limit, tile, no_edge)
        return carried

    lax.fori_loop(0, positions, prepare, 0)

    band_base = my_row * col_count * tile_side

    def first_level(column, carried):
        best = jnp.full(wide, far_value, jnp.float32)
        for row in range(source_rows):
            place = source_ref[row] - band_base
            inside = (place >= 0) & (place < col_count * tile_side)
            place = jnp.clip(place, 0, col_count * tile_side - 1)
            line = weights[
                (place // tile_side) * row_count + column, pl.ds(place % tile_side, 1), :
            ]
            limit = jnp.where(inside, no_edge, 0.0).astype(jnp.float32)
            best = jnp.where((sub == row) & (line < limit), line, best)
        partial[0, column, 0] = best
        return carried

    lax.fori_loop(0, row_count, first_level, 0)
    pl.semaphore_wait(barrier, row_count + col_count - 2)

    push("row", 0, lambda other: partial.at[0, other, 0], merged.at[0, my_row, 0])
    found_dist = partial[0, my_row, 0]
    for step in range(1, row_count):
        other = partner(my_row, step, row_count)
        arrived("row", 0, other, merged.at[0, other, 0])
        found_dist = jnp.minimum(found_dist, merged[0, other, 0])
    own_dist = jnp.minimum(start_dist, found_dist)
    own_paths = None
    band[0, my_col, 0] = own_dist
    push("col", 0, lambda other: band.at[0, my_col, 0], band.at[0, my_col, 0])

    def turn(position, carried):
        weights_back[position] = weights[position].T
        return carried

    def forward(level):
        near = band.at[level - 1]
        best_ref = partial.at[level]

        def clear(column, carried):
            best_ref[column, 0] = jnp.full(wide, far_value, jnp.float32)
            best_ref[column, 1] = jnp.zeros(wide, jnp.float32)
            return carried

        lax.fori_loop(0, row_count, clear, 0)

        def from_block(step, carried):
            block = partner(my_col, step, col_count)

            @pl.when(step > 0)
            def _():
                if level == 1:
                    arrived("col", 0, block, band.at[0, block, 0])
                else:
                    arrived("col", level - 1, block, band.at[level - 1, block])

            near_dist = near[block, 0]
            if level == 1:
                near_count = jnp.where(near_dist < half_far, 1.0, 0.0).astype(jnp.float32)
            else:
                near_count = near[block, 1]

            def columns(group, carried):
                first = group * row_chunk
                place = block * row_count + first
                before = [best_ref[first + t, 0] for t in range(row_chunk)]
                best = list(before)
                for u in range(tile_side):
                    wide_dist = jnp.broadcast_to(near_dist[:, u : u + 1], wide)
                    for t in range(row_chunk):
                        line = weights[place + t, u : u + 1, :]
                        best[t] = jnp.minimum(best[t], wide_dist + line)
                total = [
                    jnp.where(before[t] == best[t], best_ref[first + t, 1], 0.0)
                    for t in range(row_chunk)
                ]
                for u in range(tile_side):
                    wide_dist = jnp.broadcast_to(near_dist[:, u : u + 1], wide)
                    wide_count = jnp.broadcast_to(near_count[:, u : u + 1], wide)
                    for t in range(row_chunk):
                        line = weights[place + t, u : u + 1, :]
                        total[t] += jnp.where(wide_dist + line == best[t], wide_count, 0.0)
                for t in range(row_chunk):
                    best_ref[first + t, 0] = best[t]
                    best_ref[first + t, 1] = total[t]
                return carried

            return lax.fori_loop(0, row_count // row_chunk, columns, carried)

        lax.fori_loop(0, col_count, from_block, 0)
        push("row", level, lambda other: best_ref.at[other], merged.at[level, my_row])
        found_dist = best_ref[my_row, 0]
        found_count = best_ref[my_row, 1]
        for step in range(1, row_count):
            other = partner(my_row, step, row_count)
            arrived("row", level, other, merged.at[level, other])
            other_dist = merged[level, other, 0]
            both = jnp.minimum(found_dist, other_dist)
            found_count = jnp.where(found_dist == both, found_count, 0.0) + jnp.where(
                other_dist == both, merged[level, other, 1], 0.0
            )
            found_dist = both
        own_dist = jnp.minimum(start_dist, found_dist)
        own_paths = source_ones + jnp.where(found_dist == own_dist, found_count, 0.0)
        return own_dist, own_paths

    lax.fori_loop(0, positions, turn, 0)
    for level in range(1, LEVELS):
        own_dist, own_paths = forward(level)
        if level < LEVELS - 1:
            band[level, my_col, 0] = own_dist
            band[level, my_col, 1] = own_paths
            push("col", level, lambda other: band.at[level, my_col], band.at[level, my_col])

    last = LEVELS - 1
    dependency = jnp.zeros(wide, jnp.float32)
    for back in range(BACK):
        coefficient = jnp.where(
            own_paths > 0.5, (1.0 + dependency) / jnp.maximum(own_paths, 1.0), 0.0
        )
        if back == 0:
            band[last, my_col, 0] = own_dist
            push("col", last, lambda other: band.at[last, my_col, 0], band.at[last, my_col, 0])
            lower[0, my_row, 0] = own_dist
            lower[0, my_row, 1] = coefficient
            push("row", LEVELS, lambda other: lower.at[0, my_row], lower.at[0, my_row])
            dist_out[...] = jnp.where(own_dist < half_far, own_dist, -1.0)
            path_out[...] = own_paths
        else:
            lower[back, my_row, 1] = coefficient
            push(
                "row",
                LEVELS + back,
                lambda other: lower.at[back, my_row, 1],
                lower.at[back, my_row, 1],
            )

        def clear(block, carried):
            sums_out[back, block] = jnp.zeros(wide, jnp.float32)
            return carried

        lax.fori_loop(0, col_count, clear, 0)
        if back == 0:
            for step in range(1, col_count):
                other = partner(my_col, step, col_count)
                arrived("col", last, other, band.at[last, other, 0])

        def from_column(step, carried):
            column = partner(my_row, step, row_count)

            @pl.when(step > 0)
            def _():
                if back == 0:
                    arrived("row", LEVELS, column, lower.at[0, column])
                else:
                    arrived("row", LEVELS + back, column, lower.at[back, column, 1])

            low_dist = lower[0, column, 0]
            low_coef = lower[back, column, 1]

            def blocks(group, carried):
                first = group * col_chunk
                upper = [band[last, first + t, 0] for t in range(col_chunk)]
                total = [sums_out[back, first + t] for t in range(col_chunk)]
                for v in range(tile_side):
                    wide_dist = jnp.broadcast_to(low_dist[:, v : v + 1], wide)
                    wide_coef = jnp.broadcast_to(low_coef[:, v : v + 1], wide)
                    for t in range(col_chunk):
                        line = weights_back[(first + t) * row_count + column, v : v + 1, :]
                        total[t] += jnp.where(upper[t] + line == wide_dist, wide_coef, 0.0)
                for t in range(col_chunk):
                    sums_out[back, first + t] = total[t]
                return carried

            return lax.fori_loop(0, col_count // col_chunk, blocks, carried)

        lax.fori_loop(0, row_count, from_column, 0)
        stage = LEVELS + back
        push("col", stage, lambda other: sums_out.at[back, other], sums_in.at[back, my_col])
        summed = sums_out[back, my_col]
        for step in range(1, col_count):
            other = partner(my_col, step, col_count)
            arrived("col", stage, other, sums_in.at[back, other])
            summed += sums_in[back, other]
        dependency = own_paths * summed
    cent_out[...] = (
        jnp.sum(jnp.where(own_source, 0.0, dependency), axis=0, keepdims=True) / source_rows
    )
    for copy in pending:
        copy.wait_send()


def solution(mesh):
    row_count = mesh.shape["row"]
    col_count = mesh.shape["col"]
    stages = LEVELS + BACK

    def per_device(tiles, tile_index, tile_count, sources):
        slot_total, tile_side = tiles.shape[0], tiles.shape[1]
        source_rows = sources.shape[0]
        wide = (source_rows, tile_side)
        positions = row_count * col_count
        vector = pl.BlockSpec(memory_space=pltpu.VMEM)
        scalar = pl.BlockSpec(memory_space=pltpu.SMEM)
        distance, paths, centrality = pl.pallas_call(
            functools.partial(body, row_count, col_count),
            out_shape=(
                jax.ShapeDtypeStruct(wide, jnp.float32),
                jax.ShapeDtypeStruct(wide, jnp.float32),
                jax.ShapeDtypeStruct((1, tile_side), jnp.float32),
            ),
            in_specs=[scalar, scalar, scalar, pl.BlockSpec(memory_space=pl.ANY)],
            out_specs=(vector, vector, vector),
            scratch_shapes=[
                pltpu.VMEM((slot_total, tile_side, tile_side), jnp.float32),
                pltpu.SMEM((positions,), jnp.int32),
                pltpu.VMEM((positions, tile_side, tile_side), jnp.float32),
                pltpu.VMEM((positions, tile_side, tile_side), jnp.float32),
                pltpu.VMEM((LEVELS, row_count, 2) + wide, jnp.float32),
                pltpu.VMEM((LEVELS, row_count, 2) + wide, jnp.float32),
                pltpu.VMEM((LEVELS, col_count, 2) + wide, jnp.float32),
                pltpu.VMEM((BACK, row_count, 2) + wide, jnp.float32),
                pltpu.VMEM((BACK, col_count) + wide, jnp.float32),
                pltpu.VMEM((BACK, col_count) + wide, jnp.float32),
                pltpu.SemaphoreType.DMA,
                pltpu.SemaphoreType.DMA((stages, row_count)),
                pltpu.SemaphoreType.DMA((stages, row_count)),
                pltpu.SemaphoreType.DMA((stages, col_count)),
                pltpu.SemaphoreType.DMA((stages, col_count)),
            ],
            compiler_params=pltpu.CompilerParams(
                collective_id=0,
                has_side_effects=True,
            ),
        )(tile_index, tile_count, sources, tiles)
        return distance, paths, centrality.reshape(tile_side)

    in_specs = (
        P(("groups", "row", "col"), None, None),
        P(("groups", "row", "col"), None),
        P(("groups", "row", "col")),
        P("groups"),
    )
    out_specs = (
        P("groups", ("row", "col")),
        P("groups", ("row", "col")),
        P(("groups", "row", "col")),
    )
    return jax.shard_map(
        per_device, mesh=mesh, in_specs=in_specs, out_specs=out_specs, check_vma=False
    )
```

```python
import functools

import jax
import jax.numpy as jnp
from jax import lax
from jax.experimental import pallas as pl
from jax.experimental.pallas import tpu as pltpu
from jax.sharding import PartitionSpec as P

LEVELS = 3
BACK = 2
CHUNK = 4

far_value = 1000000.0
no_edge = 2000000.0
half_far = 500000.0


def partner(me, step, count):
    if count & (count - 1):
        return (me + step) % count
    total = 0
    bit = 1
    while bit < count:
        total = total + ((me // bit) % 2 + (step // bit) % 2) % 2 * bit
        bit *= 2
    return total


def body(
    row_count,
    col_count,
    index_ref,
    count_ref,
    source_ref,
    tiles_ref,
    packed,
    raw,
    place_ref,
    weights,
    weights_back,
    partial,
    merged,
    band,
    lower,
    sums_out,
    sums_in,
    load_sem,
    row_send,
    row_recv,
    col_send,
    col_recv,
):
    slot_total, tile_side = raw.shape[0], raw.shape[1]
    source_rows = source_ref.shape[0]
    my_row = lax.axis_index("row")
    my_col = lax.axis_index("col")
    positions = row_count * col_count
    row_chunk = CHUNK if row_count % CHUNK == 0 else 1
    col_chunk = CHUNK if col_count % CHUNK == 0 else 1
    wide = (source_rows, tile_side)
    pending = []

    load = pltpu.make_async_copy(tiles_ref, raw, load_sem)
    load.start()
    barrier = pltpu.get_barrier_semaphore()
    for axis, me, count in (("row", my_row, row_count), ("col", my_col, col_count)):
        for step in range(1, count):
            pl.semaphore_signal(
                barrier,
                inc=1,
                device_id={axis: partner(me, step, count)},
                device_id_type=pl.DeviceIdType.MESH,
            )

    def push(axis, stage, source_of, target):
        me, count = (my_row, row_count) if axis == "row" else (my_col, col_count)
        send, recv = (row_send, row_recv) if axis == "row" else (col_send, col_recv)
        for step in reversed(range(1, count)):
            other = partner(me, step, count)
            copy = pltpu.make_async_remote_copy(
                src_ref=source_of(other),
                dst_ref=target,
                send_sem=send.at[stage, step],
                recv_sem=recv.at[stage, me],
                device_id={axis: other},
                device_id_type=pl.DeviceIdType.MESH,
            )
            copy.start()
            pending.append(copy)

    def arrived(axis, stage, other, target):
        send, recv = (row_send, row_recv) if axis == "row" else (col_send, col_recv)
        pltpu.make_async_remote_copy(
            src_ref=target,
            dst_ref=target,
            send_sem=send.at[stage, 0],
            recv_sem=recv.at[stage, other],
            device_id={axis: other},
            device_id_type=pl.DeviceIdType.MESH,
        ).wait_recv()

    live_count = count_ref[0]
    holds = []
    for slot in range(slot_total):
        position = index_ref[0, slot] * row_count + index_ref[1, slot]
        holds.append(jnp.where(slot < live_count, position, -1))

    def find_slot(position, carried):
        found = jnp.int32(-1)
        for slot in range(slot_total):
            found = jnp.where(holds[slot] == position, jnp.int32(slot), found)
        place_ref[position] = found
        return carried

    lax.fori_loop(0, positions, find_slot, 0)

    lane = lax.broadcasted_iota(jnp.int32, wide, 1)
    sub = lax.broadcasted_iota(jnp.int32, wide, 0)
    own_base = (my_row * col_count + my_col) * tile_side
    wanted = jnp.full(wide, -1, jnp.int32)
    for row in range(source_rows):
        wanted = jnp.where(sub == row, source_ref[row] - own_base, wanted)
    own_source = lane == wanted
    start_dist = jnp.where(own_source, 0.0, far_value).astype(jnp.float32)
    source_ones = jnp.where(own_source, 1.0, 0.0).astype(jnp.float32)

    load.wait()

    band_base = my_row * col_count * tile_side

    def first_level(column, carried):
        best = jnp.full(wide, far_value, jnp.float32)
        for row in range(source_rows):
            place = source_ref[row] - band_base
            inside = (place >= 0) & (place < col_count * tile_side)
            place = jnp.clip(place, 0, col_count * tile_side - 1)
            slot = place_ref[(place // tile_side) * row_count + column]
            line = raw[jnp.maximum(slot, 0), pl.ds(place % tile_side, 1), :]
            limit = jnp.where(inside & (slot >= 0), 0.0, far_value).astype(jnp.float32)
            best = jnp.where((sub == row) & (line > limit), line, best)
        partial[0, column, 0] = best
        return carried

    lax.fori_loop(0, row_count, first_level, 0)
    pl.semaphore_wait(barrier, row_count + col_count - 2)

    push("row", 0, lambda other: partial.at[0, other, 0], merged.at[0, my_row, 0])
    def prepare(position, carried):
        slot = place_ref[position]
        tile = raw[jnp.maximum(slot, 0)]
        limit = jnp.where(slot >= 0, 0.0, far_value).astype(jnp.float32)
        weights[position] = jnp.where(tile > limit, tile, no_edge)
        return carried

    lax.fori_loop(0, positions, prepare, 0)

    found_dist = partial[0, my_row, 0]
    for step in range(1, row_count):
        other = partner(my_row, step, row_count)
        arrived("row", 0, other, merged.at[0, other, 0])
        found_dist = jnp.minimum(found_dist, merged[0, other, 0])
    own_dist = jnp.minimum(start_dist, found_dist)
    own_paths = None
    band[0, my_col, 0] = own_dist
    push("col", 0, lambda other: band.at[0, my_col, 0], band.at[0, my_col, 0])

    def turn(position, carried):
        weights_back[position] = weights[position].T
        return carried

    def forward(level):
        near = band.at[level - 1]
        best_ref = partial.at[level]

        def clear(column, carried):
            best_ref[column, 0] = jnp.full(wide, far_value, jnp.float32)
            best_ref[column, 1] = jnp.zeros(wide, jnp.float32)
            return carried

        lax.fori_loop(0, row_count, clear, 0)

        def from_block(step, carried):
            block = partner(my_col, step, col_count)

            @pl.when(step > 0)
            def _():
                if level == 1:
                    arrived("col", 0, block, band.at[0, block, 0])
                else:
                    arrived("col", level - 1, block, band.at[level - 1, block])

            near_dist = near[block, 0]
            if level == 1:
                near_count = jnp.where(near_dist < half_far, 1.0, 0.0).astype(jnp.float32)
            else:
                near_count = near[block, 1]

            def columns(group, carried):
                first = group * row_chunk
                place = block * row_count + first
                before = [best_ref[first + t, 0] for t in range(row_chunk)]
                best = list(before)
                for u in range(tile_side):
                    wide_dist = jnp.broadcast_to(near_dist[:, u : u + 1], wide)
                    for t in range(row_chunk):
                        line = weights[place + t, u : u + 1, :]
                        best[t] = jnp.minimum(best[t], wide_dist + line)
                total = [
                    jnp.where(before[t] == best[t], best_ref[first + t, 1], 0.0)
                    for t in range(row_chunk)
                ]
                for u in range(tile_side):
                    wide_dist = jnp.broadcast_to(near_dist[:, u : u + 1], wide)
                    wide_count = jnp.broadcast_to(near_count[:, u : u + 1], wide)
                    for t in range(row_chunk):
                        line = weights[place + t, u : u + 1, :]
                        total[t] += jnp.where(wide_dist + line == best[t], wide_count, 0.0)
                for t in range(row_chunk):
                    best_ref[first + t, 0] = best[t]
                    best_ref[first + t, 1] = total[t]
                return carried

            return lax.fori_loop(0, row_count // row_chunk, columns, carried)

        lax.fori_loop(0, col_count, from_block, 0)
        push("row", level, lambda other: best_ref.at[other], merged.at[level, my_row])
        found_dist = best_ref[my_row, 0]
        found_count = best_ref[my_row, 1]
        for step in range(1, row_count):
            other = partner(my_row, step, row_count)
            arrived("row", level, other, merged.at[level, other])
            other_dist = merged[level, other, 0]
            both = jnp.minimum(found_dist, other_dist)
            found_count = jnp.where(found_dist == both, found_count, 0.0) + jnp.where(
                other_dist == both, merged[level, other, 1], 0.0
            )
            found_dist = both
        own_dist = jnp.minimum(start_dist, found_dist)
        own_paths = source_ones + jnp.where(found_dist == own_dist, found_count, 0.0)
        return own_dist, own_paths

    lax.fori_loop(0, positions, turn, 0)
    for level in range(1, LEVELS):
        own_dist, own_paths = forward(level)
        if level < LEVELS - 1:
            band[level, my_col, 0] = own_dist
            band[level, my_col, 1] = own_paths
            push("col", level, lambda other: band.at[level, my_col], band.at[level, my_col])

    last = LEVELS - 1
    dependency = jnp.zeros(wide, jnp.float32)
    for back in range(BACK):
        coefficient = jnp.where(
            own_paths > 0.5, (1.0 + dependency) / jnp.maximum(own_paths, 1.0), 0.0
        )
        if back == 0:
            band[last, my_col, 0] = own_dist
            push("col", last, lambda other: band.at[last, my_col, 0], band.at[last, my_col, 0])
            lower[0, my_row, 0] = own_dist
            lower[0, my_row, 1] = coefficient
            push("row", LEVELS, lambda other: lower.at[0, my_row], lower.at[0, my_row])
            packed[0] = jnp.where(own_dist < half_far, own_dist, -1.0)
            packed[1] = own_paths
        else:
            lower[back, my_row, 1] = coefficient
            push(
                "row",
                LEVELS + back,
                lambda other: lower.at[back, my_row, 1],
                lower.at[back, my_row, 1],
            )

        def clear(block, carried):
            sums_out[back, block] = jnp.zeros(wide, jnp.float32)
            return carried

        if back == 0:
            for step in range(1, row_count):
                other = partner(my_row, step, row_count)
                arrived("row", LEVELS, other, lower.at[0, other])

            def from_block(step, carried):
                block = partner(my_col, step, col_count)

                @pl.when(step > 0)
                def _():
                    arrived("col", last, block, band.at[last, block, 0])

                upper = band[last, block, 0]

                def columns(group, total):
                    first = group * row_chunk
                    place = block * row_count + first
                    low_dist = [lower[0, first + t, 0] for t in range(row_chunk)]
                    low_coef = [lower[0, first + t, 1] for t in range(row_chunk)]
                    parts = [jnp.zeros(wide, jnp.float32)] * row_chunk
                    for v in range(tile_side):
                        for t in range(row_chunk):
                            line = weights_back[place + t, v : v + 1, :]
                            wide_dist = jnp.broadcast_to(low_dist[t][:, v : v + 1], wide)
                            wide_coef = jnp.broadcast_to(low_coef[t][:, v : v + 1], wide)
                            parts[t] += jnp.where(upper + line == wide_dist, wide_coef, 0.0)
                    return total + sum(parts[1:], parts[0])

                sums_out[0, block] = lax.fori_loop(
                    0, row_count // row_chunk, columns, jnp.zeros(wide, jnp.float32)
                )
                return carried

            lax.fori_loop(0, col_count, from_block, 0)
        else:
            lax.fori_loop(0, col_count, clear, 0)

            def from_column(step, carried):
                column = partner(my_row, step, row_count)

                @pl.when(step > 0)
                def _():
                    arrived("row", LEVELS + back, column, lower.at[back, column, 1])

                low_dist = lower[0, column, 0]
                low_coef = lower[back, column, 1]

                def blocks(group, carried):
                    first = group * col_chunk
                    upper = [band[last, first + t, 0] for t in range(col_chunk)]
                    total = [sums_out[back, first + t] for t in range(col_chunk)]
                    for v in range(tile_side):
                        wide_dist = jnp.broadcast_to(low_dist[:, v : v + 1], wide)
                        wide_coef = jnp.broadcast_to(low_coef[:, v : v + 1], wide)
                        for t in range(col_chunk):
                            line = weights_back[(first + t) * row_count + column, v : v + 1, :]
                            total[t] += jnp.where(upper[t] + line == wide_dist, wide_coef, 0.0)
                    for t in range(col_chunk):
                        sums_out[back, first + t] = total[t]
                    return carried

                return lax.fori_loop(0, col_count // col_chunk, blocks, carried)

            lax.fori_loop(0, row_count, from_column, 0)
        stage = LEVELS + back
        push("col", stage, lambda other: sums_out.at[back, other], sums_in.at[back, my_col])
        summed = sums_out[back, my_col]
        for step in range(1, col_count):
            other = partner(my_col, step, col_count)
            arrived("col", stage, other, sums_in.at[back, other])
            summed += sums_in[back, other]
        dependency = own_paths * summed
    packed[2] = jnp.where(own_source, 0.0, dependency)
    for copy in pending:
        copy.wait_send()


def unpack(packed, dist_out, path_out, cent_out):
    dist_out[...] = packed[0]
    path_out[...] = packed[1]
    cent_out[...] = jnp.sum(packed[2], axis=0, keepdims=True) / packed.shape[1]


def solution(mesh):
    row_count = mesh.shape["row"]
    col_count = mesh.shape["col"]
    stages = LEVELS + BACK

    def per_device(tiles, tile_index, tile_count, sources):
        slot_total, tile_side = tiles.shape[0], tiles.shape[1]
        source_rows = sources.shape[0]
        wide = (source_rows, tile_side)
        positions = row_count * col_count
        vector = pl.BlockSpec(memory_space=pltpu.VMEM)
        scalar = pl.BlockSpec(memory_space=pltpu.SMEM)
        packed = pl.pallas_call(
            functools.partial(body, row_count, col_count),
            out_shape=jax.ShapeDtypeStruct((3,) + wide, jnp.float32),
            in_specs=[scalar, scalar, scalar, pl.BlockSpec(memory_space=pl.ANY)],
            out_specs=vector,
            scratch_shapes=[
                pltpu.VMEM((slot_total, tile_side, tile_side), jnp.float32),
                pltpu.SMEM((positions,), jnp.int32),
                pltpu.VMEM((positions, tile_side, tile_side), jnp.float32),
                pltpu.VMEM((positions, tile_side, tile_side), jnp.float32),
                pltpu.VMEM((LEVELS, row_count, 2) + wide, jnp.float32),
                pltpu.VMEM((LEVELS, row_count, 2) + wide, jnp.float32),
                pltpu.VMEM((LEVELS, col_count, 2) + wide, jnp.float32),
                pltpu.VMEM((BACK, row_count, 2) + wide, jnp.float32),
                pltpu.VMEM((BACK, col_count) + wide, jnp.float32),
                pltpu.VMEM((BACK, col_count) + wide, jnp.float32),
                pltpu.SemaphoreType.DMA,
                pltpu.SemaphoreType.DMA((stages, row_count)),
                pltpu.SemaphoreType.DMA((stages, row_count)),
                pltpu.SemaphoreType.DMA((stages, col_count)),
                pltpu.SemaphoreType.DMA((stages, col_count)),
            ],
            compiler_params=pltpu.CompilerParams(
                collective_id=0,
                has_side_effects=True,
            ),
        )(tile_index.T, tile_count, sources, tiles)
        distance, paths, centrality = pl.pallas_call(
            unpack,
            out_shape=(
                jax.ShapeDtypeStruct(wide, jnp.float32),
                jax.ShapeDtypeStruct(wide, jnp.float32),
                jax.ShapeDtypeStruct((1, tile_side), jnp.float32),
            ),
            in_specs=[vector],
            out_specs=(vector, vector, vector),
        )(packed)
        return distance, paths, centrality.reshape(tile_side)

    in_specs = (
        P(("groups", "row", "col"), None, None),
        P(("groups", "row", "col"), None),
        P(("groups", "row", "col")),
        P("groups"),
    )
    out_specs = (
        P("groups", ("row", "col")),
        P("groups", ("row", "col")),
        P(("groups", "row", "col")),
    )
    return jax.shard_map(
        per_device, mesh=mesh, in_specs=in_specs, out_specs=out_specs, check_vma=False
    )
```

```python
import functools

import jax
import jax.numpy as jnp
from jax import lax
from jax.experimental import pallas as pl
from jax.experimental.pallas import tpu as pltpu
from jax.sharding import PartitionSpec as P

LEVELS = 3
BACK = 2
CHUNK = 4

far_value = 1000000.0
no_edge = 2000000.0
half_far = 500000.0


def partner(me, step, count):
    if count & (count - 1):
        return (me + step) % count
    total = 0
    bit = 1
    while bit < count:
        total = total + ((me // bit) % 2 + (step // bit) % 2) % 2 * bit
        bit *= 2
    return total


def body(
    row_count,
    col_count,
    index_ref,
    count_ref,
    source_ref,
    tiles_ref,
    packed,
    raw,
    place_ref,
    weights,
    weights_back,
    partial,
    inbox,
    full,
    band,
    lower,
    sums_out,
    sums_all,
    sums_in,
    load_sem,
    all_send,
    all_recv,
    full_send,
    full_recv,
    col_send,
    col_recv,
):
    slot_total, tile_side = raw.shape[0], raw.shape[1]
    source_rows = source_ref.shape[0]
    my_row = lax.axis_index("row")
    my_col = lax.axis_index("col")
    positions = row_count * col_count
    row_chunk = CHUNK if row_count % CHUNK == 0 else 1
    col_chunk = CHUNK if col_count % CHUNK == 0 else 1
    wide = (source_rows, tile_side)
    pending = []

    def others():
        for col_step in reversed(range(col_count)):
            for row_step in reversed(range(row_count)):
                if row_step or col_step:
                    yield (
                        partner(my_row, row_step, row_count),
                        partner(my_col, col_step, col_count),
                        row_step,
                        col_step,
                    )

    load = pltpu.make_async_copy(tiles_ref, raw, load_sem)
    load.start()
    barrier = pltpu.get_barrier_semaphore()
    for other_row, other_col, _, _ in others():
        pl.semaphore_signal(
            barrier,
            inc=1,
            device_id={"row": other_row, "col": other_col},
            device_id_type=pl.DeviceIdType.MESH,
        )

    def start(source, target, send, recv, device):
        copy = pltpu.make_async_remote_copy(
            src_ref=source,
            dst_ref=target,
            send_sem=send,
            recv_sem=recv,
            device_id=device,
            device_id_type=pl.DeviceIdType.MESH,
        )
        copy.start()
        pending.append(copy)

    def push_all(stage, source_of, target):
        for other_row, other_col, row_step, col_step in others():
            start(
                source_of(other_row, other_col),
                target,
                all_send.at[stage, row_step, col_step],
                all_recv.at[stage, my_row, my_col],
                {"row": other_row, "col": other_col},
            )

    def arrived(target, recv, device):
        pltpu.make_async_remote_copy(
            src_ref=target,
            dst_ref=target,
            send_sem=load_sem,
            recv_sem=recv,
            device_id=device,
            device_id_type=pl.DeviceIdType.MESH,
        ).wait_recv()

    def source_mask(base):
        wanted = jnp.full(wide, -1, jnp.int32)
        for row in range(source_rows):
            wanted = jnp.where(sub == row, source_ref[row] - base, wanted)
        return lane == wanted

    def settle(found_dist, found_count, is_source):
        start_dist = jnp.where(is_source, 0.0, far_value).astype(jnp.float32)
        settled = jnp.minimum(start_dist, found_dist)
        ones = jnp.where(is_source, 1.0, 0.0).astype(jnp.float32)
        return settled, ones + jnp.where(found_dist == settled, found_count, 0.0)

    def combine(pieces):
        best, total = pieces[0]
        for other_best, other_total in pieces[1:]:
            both = jnp.minimum(best, other_best)
            total = jnp.where(best == both, total, 0.0) + jnp.where(
                other_best == both, other_total, 0.0
            )
            best = both
        return best, total

    live_count = count_ref[0]
    holds = []
    for slot in range(slot_total):
        position = index_ref[0, slot] * row_count + index_ref[1, slot]
        holds.append(jnp.where(slot < live_count, position, -1))

    def find_slot(position, carried):
        found = jnp.int32(-1)
        for slot in range(slot_total):
            found = jnp.where(holds[slot] == position, jnp.int32(slot), found)
        place_ref[position] = found
        return carried

    lax.fori_loop(0, positions, find_slot, 0)

    lane = lax.broadcasted_iota(jnp.int32, wide, 1)
    sub = lax.broadcasted_iota(jnp.int32, wide, 0)
    load.wait()

    band_base = my_row * col_count * tile_side

    def first_level(column, carried):
        best = jnp.full(wide, far_value, jnp.float32)
        for row in range(source_rows):
            place = source_ref[row] - band_base
            inside = (place >= 0) & (place < col_count * tile_side)
            place = jnp.clip(place, 0, col_count * tile_side - 1)
            slot = place_ref[(place // tile_side) * row_count + column]
            line = raw[jnp.maximum(slot, 0), pl.ds(place % tile_side, 1), :]
            limit = jnp.where(inside & (slot >= 0), 0.0, far_value).astype(jnp.float32)
            best = jnp.where((sub == row) & (line > limit), line, best)
        partial[0, column, 0] = best
        return carried

    lax.fori_loop(0, row_count, first_level, 0)
    inbox[0, my_col, my_row, 0] = partial[0, my_row, 0]
    pl.semaphore_wait(barrier, row_count * col_count - 1)
    push_all(
        0, lambda other_row, other_col: partial.at[0, other_row, 0], inbox.at[0, my_col, my_row, 0]
    )

    def prepare(position, carried):
        slot = place_ref[position]
        tile = raw[jnp.maximum(slot, 0)]
        limit = jnp.where(slot >= 0, 0.0, far_value).astype(jnp.float32)
        weights[position] = jnp.where(tile > limit, tile, no_edge)
        return carried

    lax.fori_loop(0, positions, prepare, 0)

    def turn(position, carried):
        weights_back[position] = weights[position].T
        return carried

    def band_block(stage, block, step):
        for row_step in range(row_count):
            giver = partner(my_row, row_step, row_count)

            def wait():
                piece = inbox.at[stage, block, giver]
                arrived(
                    piece.at[0] if stage in (0, LEVELS - 1) else piece,
                    all_recv.at[stage, giver, block],
                    {"row": giver, "col": block},
                )

            if row_step == 0:
                pl.when(step > 0)(wait)
            else:
                wait()
        is_source = source_mask((my_row * col_count + block) * tile_side)
        if stage in (0, LEVELS - 1):
            best = inbox[stage, block, 0, 0]
            for giver in range(1, row_count):
                best = jnp.minimum(best, inbox[stage, block, giver, 0])
            best = jnp.where(is_source, 0.0, best)
            return best, jnp.where(best < half_far, 1.0, 0.0).astype(jnp.float32)
        found = combine([(inbox[stage, block, g, 0], inbox[stage, block, g, 1]) for g in range(row_count)])
        return settle(*found, is_source)

    def forward(level):
        best_ref = partial.at[level]

        def clear(column, carried):
            best_ref[column, 0] = jnp.full(wide, far_value, jnp.float32)
            best_ref[column, 1] = jnp.zeros(wide, jnp.float32)
            return carried

        lax.fori_loop(0, row_count, clear, 0)

        def from_block(step, carried):
            block = partner(my_col, step, col_count)

            near_dist, near_count = band_block(level - 1, block, step)

            def columns(group, carried):
                first = group * row_chunk
                place = block * row_count + first
                before = [best_ref[first + t, 0] for t in range(row_chunk)]
                best = list(before)
                for u in range(tile_side):
                    wide_dist = jnp.broadcast_to(near_dist[:, u : u + 1], wide)
                    for t in range(row_chunk):
                        line = weights[place + t, u : u + 1, :]
                        best[t] = jnp.minimum(best[t], wide_dist + line)
                total = [
                    jnp.where(before[t] == best[t], best_ref[first + t, 1], 0.0)
                    for t in range(row_chunk)
                ]
                for u in range(tile_side):
                    wide_dist = jnp.broadcast_to(near_dist[:, u : u + 1], wide)
                    wide_count = jnp.broadcast_to(near_count[:, u : u + 1], wide)
                    for t in range(row_chunk):
                        line = weights[place + t, u : u + 1, :]
                        total[t] += jnp.where(wide_dist + line == best[t], wide_count, 0.0)
                for t in range(row_chunk):
                    best_ref[first + t, 0] = best[t]
                    best_ref[first + t, 1] = total[t]
                return carried

            return lax.fori_loop(0, row_count // row_chunk, columns, carried)

        lax.fori_loop(0, col_count, from_block, 0)
        inbox[level, my_col, my_row] = best_ref[my_row]
        if level == LEVELS - 1:
            push_all(
                level,
                lambda other_row, other_col: best_ref.at[other_row, 0],
                inbox.at[level, my_col, my_row, 0],
            )
        else:
            push_all(
                level,
                lambda other_row, other_col: best_ref.at[other_row],
                inbox.at[level, my_col, my_row],
            )

    lax.fori_loop(0, positions, turn, 0)
    for level in range(1, LEVELS):
        forward(level)

    last = LEVELS - 1
    full[my_row] = partial[last]
    for row_step in reversed(range(1, row_count)):
        other = partner(my_row, row_step, row_count)
        start(
            partial.at[last],
            full.at[my_row],
            full_send.at[row_step],
            full_recv.at[my_row],
            {"row": other, "col": my_col},
        )
    for row_step in range(1, row_count):
        other = partner(my_row, row_step, row_count)
        arrived(full.at[other], full_recv.at[other], {"row": other, "col": my_col})

    def settle_column(column, carried):
        found = combine([(full[g, column, 0], full[g, column, 1]) for g in range(row_count)])
        base = (column * col_count + my_col) * tile_side
        lower[0, column], lower[1, column] = settle(*found, source_mask(base))
        return carried

    lax.fori_loop(0, row_count, settle_column, 0)
    own_dist = lower[0, my_row]
    own_paths = lower[1, my_row]
    packed[0] = jnp.where(own_dist < half_far, own_dist, -1.0)
    packed[1] = own_paths

    def settle_block(step, carried):
        block = partner(my_col, step, col_count)
        band[block] = band_block(last, block, step)[0]
        return carried

    lax.fori_loop(0, col_count, settle_block, 0)

    for back in range(BACK):

        def clear(block, carried):
            sums_out[back, block] = jnp.zeros(wide, jnp.float32)
            return carried

        lax.fori_loop(0, col_count, clear, 0)

        def from_column(step, carried):
            column = partner(my_row, step, row_count)
            low_dist = lower[0, column]
            low_paths = lower[1, column]
            if back == 0:
                dependency = 0.0
            else:
                summed = jnp.zeros(wide, jnp.float32)
                for col_step in range(col_count):
                    giver = partner(my_col, col_step, col_count)

                    def wait():
                        arrived(
                            sums_all.at[column, giver],
                            all_recv.at[LEVELS, column, giver],
                            {"row": column, "col": giver},
                        )

                    if col_step == 0:
                        pl.when(step > 0)(wait)
                    else:
                        wait()
                for giver in range(col_count):
                    summed += sums_all[column, giver]
                dependency = low_paths * summed
            low_coef = jnp.where(
                low_paths > 0.5, (1.0 + dependency) / jnp.maximum(low_paths, 1.0), 0.0
            )

            def blocks(group, carried):
                first = group * col_chunk
                upper = [band[first + t] for t in range(col_chunk)]
                total = [sums_out[back, first + t] for t in range(col_chunk)]
                for v in range(tile_side):
                    wide_dist = jnp.broadcast_to(low_dist[:, v : v + 1], wide)
                    wide_coef = jnp.broadcast_to(low_coef[:, v : v + 1], wide)
                    for t in range(col_chunk):
                        line = weights_back[(first + t) * row_count + column, v : v + 1, :]
                        total[t] += jnp.where(upper[t] + line == wide_dist, wide_coef, 0.0)
                for t in range(col_chunk):
                    sums_out[back, first + t] = total[t]
                return carried

            return lax.fori_loop(0, col_count // col_chunk, blocks, carried)

        lax.fori_loop(0, row_count, from_column, 0)
        if back == 0:
            sums_all[my_row, my_col] = sums_out[0, my_col]
            push_all(
                LEVELS,
                lambda other_row, other_col: sums_out.at[0, other_col],
                sums_all.at[my_row, my_col],
            )
    for col_step in reversed(range(1, col_count)):
        other = partner(my_col, col_step, col_count)
        start(
            sums_out.at[1, other],
            sums_in.at[my_col],
            col_send.at[col_step],
            col_recv.at[my_col],
            {"row": my_row, "col": other},
        )
    summed = sums_out[1, my_col]
    for col_step in range(1, col_count):
        other = partner(my_col, col_step, col_count)
        arrived(sums_in.at[other], col_recv.at[other], {"row": my_row, "col": other})
        summed += sums_in[other]
    own_source = source_mask((my_row * col_count + my_col) * tile_side)
    packed[2] = jnp.where(own_source, 0.0, own_paths * summed)
    for copy in pending:
        copy.wait_send()


def unpack(packed, dist_out, path_out, cent_out):
    dist_out[...] = packed[0]
    path_out[...] = packed[1]
    cent_out[...] = jnp.sum(packed[2], axis=0, keepdims=True) / packed.shape[1]


def solution(mesh):
    row_count = mesh.shape["row"]
    col_count = mesh.shape["col"]

    def per_device(tiles, tile_index, tile_count, sources):
        slot_total, tile_side = tiles.shape[0], tiles.shape[1]
        source_rows = sources.shape[0]
        wide = (source_rows, tile_side)
        positions = row_count * col_count
        vector = pl.BlockSpec(memory_space=pltpu.VMEM)
        scalar = pl.BlockSpec(memory_space=pltpu.SMEM)
        packed = pl.pallas_call(
            functools.partial(body, row_count, col_count),
            out_shape=jax.ShapeDtypeStruct((3,) + wide, jnp.float32),
            in_specs=[scalar, scalar, scalar, pl.BlockSpec(memory_space=pl.ANY)],
            out_specs=vector,
            scratch_shapes=[
                pltpu.VMEM((slot_total, tile_side, tile_side), jnp.float32),
                pltpu.SMEM((positions,), jnp.int32),
                pltpu.VMEM((positions, tile_side, tile_side), jnp.float32),
                pltpu.VMEM((positions, tile_side, tile_side), jnp.float32),
                pltpu.VMEM((LEVELS, row_count, 2) + wide, jnp.float32),
                pltpu.VMEM((LEVELS, col_count, row_count, 2) + wide, jnp.float32),
                pltpu.VMEM((row_count, row_count, 2) + wide, jnp.float32),
                pltpu.VMEM((col_count,) + wide, jnp.float32),
                pltpu.VMEM((2, row_count) + wide, jnp.float32),
                pltpu.VMEM((BACK, col_count) + wide, jnp.float32),
                pltpu.VMEM((row_count, col_count) + wide, jnp.float32),
                pltpu.VMEM((col_count,) + wide, jnp.float32),
                pltpu.SemaphoreType.DMA,
                pltpu.SemaphoreType.DMA((LEVELS + 1, row_count, col_count)),
                pltpu.SemaphoreType.DMA((LEVELS + 1, row_count, col_count)),
                pltpu.SemaphoreType.DMA((row_count,)),
                pltpu.SemaphoreType.DMA((row_count,)),
                pltpu.SemaphoreType.DMA((col_count,)),
                pltpu.SemaphoreType.DMA((col_count,)),
            ],
            compiler_params=pltpu.CompilerParams(
                collective_id=0,
                has_side_effects=True,
            ),
        )(tile_index.T, tile_count, sources, tiles)
        distance, paths, centrality = pl.pallas_call(
            unpack,
            out_shape=(
                jax.ShapeDtypeStruct(wide, jnp.float32),
                jax.ShapeDtypeStruct(wide, jnp.float32),
                jax.ShapeDtypeStruct((1, tile_side), jnp.float32),
            ),
            in_specs=[vector],
            out_specs=(vector, vector, vector),
        )(packed)
        return distance, paths, centrality.reshape(tile_side)

    in_specs = (
        P(("groups", "row", "col"), None, None),
        P(("groups", "row", "col"), None),
        P(("groups", "row", "col")),
        P("groups"),
    )
    out_specs = (
        P("groups", ("row", "col")),
        P("groups", ("row", "col")),
        P(("groups", "row", "col")),
    )
    return jax.shard_map(
        per_device, mesh=mesh, in_specs=in_specs, out_specs=out_specs, check_vma=False
    )
```
